32 devices in a mesh: gx: 8 (over y, x, core), gy: 4 (over z).
Axes of the slice: x: 2, y: 2, z: 4, core: 2. Of those that a mesh axis runs over, the one named last changes fastest.
Arguments:
- history: bfloat16 [4, 2048, 2048], P(None, 'gx', 'gy'), may hold values from -6 to 6
- start_x: float32 [2048, 256], P('gx'), may hold values from -6 to 6
- start_y: float32 [2048, 256], P('gy'), may hold values from -6 to 6
Outputs:
- core: float32 [4, 256, 256], P(None, 'gx', 'gy')
The draws below stay inside these ranges and needn't reach their ends.
All inputs are finite; a program needn't handle non-finite values.
Results may differ from the reference program's by a relative error of at most 0.0027.
Values may be sent and summed in bfloat16 or wider, within the bound.
A program may use at most 128 MiB of HBM per device.

```python
import jax
import jax.numpy as jnp
from jax import lax

NX = 2048
NY = 2048
RANK = 256
SLABS = 4
ITERS = 3


def level_of(stream_key, extent, pieces, least, high):
    def one(dim, parts):
        steps = jax.random.uniform(jax.random.fold_in(jax.random.fold_in(stream_key, 6), dim), (parts,), jnp.float32, least / len(pieces), high / len(pieces))
        return jnp.repeat(jnp.exp(steps), extent[dim] // parts).reshape((-1,) + (1,) * (len(extent) - dim - 1))

    gain = one(*pieces[0])
    for cut in pieces[1:]:
        gain = gain * one(*cut)
    return gain


def noise(key, extent, scale, limit, split=(), kind=jnp.bfloat16):
    drawn = scale * jax.random.normal(key, extent, jnp.float32)
    if split:
        drawn = drawn * level_of(key, extent, split, -0.22, 0.18)
    return jnp.clip(drawn, -limit, limit).astype(kind)


def setup_inputs(seed: int = 0) -> dict:
    key_list = jax.random.split(jax.random.key(seed), 4)
    return {
        "history": noise(key_list[0], (SLABS, NX, NY), 1.0, 6.0, ((1, 8), (2, 4))),
        "start_x": noise(key_list[1], (NX, RANK), 1.0, 6.0, ((0, 8),), jnp.float32),
        "start_y": noise(key_list[2], (NY, RANK), 1.0, 6.0, ((0, 4),), jnp.float32),
    }


def subspace(gram, start):
    basis = start
    for step in range(ITERS):
        image = jnp.dot(gram.astype(jnp.float32), basis.astype(jnp.float32), precision=lax.Precision.HIGHEST, preferred_element_type=jnp.float32)
        inner = jnp.dot(image.T.astype(jnp.float32), image.astype(jnp.float32), precision=lax.Precision.HIGHEST, preferred_element_type=jnp.float32)
        lower = jnp.linalg.cholesky(inner)
        basis = lax.linalg.triangular_solve(lower, image, left_side=False, lower=True, transpose_a=True)
    return basis

def reference(history, start_x, start_y):
    data = history.astype(jnp.float32)
    by_x = jnp.transpose(data, (1, 0, 2)).reshape(NX, SLABS * NY)
    gram_x = jnp.dot(by_x.astype(jnp.float32), by_x.T.astype(jnp.float32), precision=lax.Precision.HIGHEST, preferred_element_type=jnp.float32)
    by_y = jnp.transpose(data, (2, 0, 1)).reshape(NY, SLABS * NX)
    gram_y = jnp.dot(by_y.astype(jnp.float32), by_y.T.astype(jnp.float32), precision=lax.Precision.HIGHEST, preferred_element_type=jnp.float32)
    basis_x = subspace(gram_x, start_x)
    basis_y = subspace(gram_y, start_y)
    factor_x = lax.optimization_barrier(basis_x.astype(jnp.bfloat16)).astype(jnp.float32)
    factor_y = lax.optimization_barrier(basis_y.astype(jnp.bfloat16)).astype(jnp.float32)
    partial_core = jnp.einsum('sxy,yb->sxb', data, factor_y, precision=lax.Precision.HIGHEST)
    core = jnp.einsum('xa,sxb->sab', factor_x, partial_core, precision=lax.Precision.HIGHEST)
    return core
```

```python
import functools

import jax
import jax.numpy as jnp
from jax import lax
from jax.experimental import pallas as pl
from jax.experimental.pallas import tpu as pltpu
from jax.sharding import PartitionSpec as P

ITERS = 3
BLOCK = 64
HIGH = lax.Precision.HIGH
HIGHEST = lax.Precision.HIGHEST


def eliminate(blocks):
    size = blocks[0].shape[0]
    sub = lax.broadcasted_iota(jnp.int32, (size, size), 0)
    lane = lax.broadcasted_iota(jnp.int32, (size, size), 1)
    eye = jnp.where(sub == lane, 1.0, 0.0).astype(jnp.float32)
    sub8 = lax.broadcasted_iota(jnp.int32, (8, 1), 0)
    tiles = []
    for block in blocks:
        whole = jnp.concatenate([block, eye], axis=1)
        tiles.append([whole[t * 8 : t * 8 + 8] for t in range(size // 8)])
    for k in range(size):
        home = k // 8
        for rows in tiles:
            held = rows[home]
            row = held[k % 8 : k % 8 + 1, :]
            scaled = row / row[:, k : k + 1]
            for t in range(home, size // 8):
                if t == home and k % 8 == 7:
                    continue
                col = rows[t][:, k : k + 1]
                if t == home:
                    col = jnp.where(sub8 > k % 8, col, 0.0)
                rows[t] = rows[t] - col * scaled
    out = []
    for rows in tiles:
        whole = jnp.concatenate(rows, axis=0)
        diag = jnp.sum(jnp.where(sub == lane, whole[:, :size], 0.0), axis=1, keepdims=True)
        out.append(whole[:, size:] * (1.0 / jnp.sqrt(diag)))
    return out


def mul(a, b, dims):
    return lax.dot_general(a, b, (dims, ((), ())), precision=HIGHEST, preferred_element_type=jnp.float32)


def factor_kernel(inner_ref, out_ref, work):
    modes, rank = inner_ref.shape[0], inner_ref.shape[1]
    sub = lax.broadcasted_iota(jnp.int32, (rank, rank), 0)
    lane = lax.broadcasted_iota(jnp.int32, (rank, rank), 1)
    eye = jnp.where(sub == lane, 1.0, 0.0).astype(jnp.float32)
    for m in range(modes):
        work[m, :, :rank] = inner_ref[m]
        work[m, :, rank:] = eye
    for p in range(rank // BLOCK):
        at = p * BLOCK
        inverses = eliminate([work[m, at : at + BLOCK, at : at + BLOCK] for m in range(modes)])
        for m in range(modes):
            top = mul(inverses[m], work[m, at : at + BLOCK, :], ((1,), (0,)))
            out_ref[m, at : at + BLOCK, :] = top[:, rank:]
            if at + BLOCK < rank:
                left = top[:, at + BLOCK : rank]
                work[m, at + BLOCK :, :] = work[m, at + BLOCK :, :] - mul(left, top, ((0,), (0,)))


def inverse_factors(inner):
    modes, rank = inner.shape[0], inner.shape[1]
    return pl.pallas_call(
        factor_kernel,
        out_shape=jax.ShapeDtypeStruct(inner.shape, jnp.float32),
        in_specs=[pl.BlockSpec(memory_space=pltpu.VMEM)],
        out_specs=pl.BlockSpec(memory_space=pltpu.VMEM),
        scratch_shapes=[pltpu.VMEM((modes, rank, 2 * rank), jnp.float32)],
        name="inverse_factors",
    )(inner)


def dot(a, b, precision):
    return jnp.dot(a, b, precision=precision, preferred_element_type=jnp.float32)


def on_device(history, start_x, start_y):
    nx, ny = lax.axis_size("gx"), lax.axis_size("gy")
    rows, cols, rank = history.shape[1], history.shape[2], start_x.shape[1]
    basis_x = lax.all_gather(start_x, "gx", axis=0, tiled=True)
    basis_y = lax.all_gather(start_y, "gy", axis=0, tiled=True)
    gram_x = lax.dot_general(
        history, lax.all_gather(history, "gx", axis=1, tiled=True),
        (((0, 2), (0, 2)), ((), ())), preferred_element_type=jnp.float32,
    )
    gram_y = lax.dot_general(
        history, lax.all_gather(history, "gy", axis=2, tiled=True),
        (((0, 1), (0, 1)), ((), ())), preferred_element_type=jnp.float32,
    )
    for step in range(ITERS):
        part_x = lax.psum_scatter(dot(gram_x, basis_x, HIGH), "gy", scatter_dimension=0, tiled=True)
        part_y = lax.psum_scatter(dot(gram_y, basis_y, HIGH), "gx", scatter_dimension=0, tiled=True)
        both = jnp.stack([part_x, part_y])
        both = lax.all_gather(both, "gy", axis=1)
        both = lax.all_gather(both, "gx", axis=1)
        image_x = both[0].reshape(-1, rank)
        image_y = both[1].swapaxes(0, 1).reshape(-1, rank)
        inner = jnp.stack([dot(image_x.T, image_x, HIGHEST), dot(image_y.T, image_y, HIGHEST)])
        inverse = inverse_factors(inner)
        if step == ITERS - 1:
            image_x = lax.dynamic_slice_in_dim(image_x, lax.axis_index("gx") * rows, rows, 0)
            image_y = lax.dynamic_slice_in_dim(image_y, lax.axis_index("gy") * cols, cols, 0)
        basis_x = dot(image_x, inverse[0].T, HIGH)
        basis_y = dot(image_y, inverse[1].T, HIGH)
    factor_x = basis_x.astype(jnp.bfloat16)
    factor_y = basis_y.astype(jnp.bfloat16)
    first = jnp.einsum("xa,sxy->say", factor_x, history, preferred_element_type=jnp.float32)
    first = lax.psum_scatter(first, "gx", scatter_dimension=1, tiled=True)
    second = jnp.einsum("say,yb->sab", first, factor_y.astype(jnp.float32), precision=HIGHEST)
    return lax.psum_scatter(second, "gy", scatter_dimension=2, tiled=True)


def solution(mesh):
    return jax.shard_map(
        on_device,
        mesh=mesh,
        in_specs=(P(None, "gx", "gy"), P("gx", None), P("gy", None)),
        out_specs=P(None, "gx", "gy"),
        check_vma=False,
    )
```

```python
import functools

import jax
import jax.numpy as jnp
from jax import lax
from jax.experimental import pallas as pl
from jax.experimental.pallas import tpu as pltpu
from jax.sharding import PartitionSpec as P

ITERS = 3
BLOCK = 64
HIGH = lax.Precision.HIGH
HIGHEST = lax.Precision.HIGHEST


def eliminate(blocks):
    size = blocks[0].shape[0]
    sub = lax.broadcasted_iota(jnp.int32, (size, size), 0)
    lane = lax.broadcasted_iota(jnp.int32, (size, size), 1)
    eye = jnp.where(sub == lane, 1.0, 0.0).astype(jnp.float32)
    sub8 = lax.broadcasted_iota(jnp.int32, (8, 1), 0)
    tiles = []
    for block in blocks:
        whole = jnp.concatenate([block, eye], axis=1)
        tiles.append([whole[t * 8 : t * 8 + 8] for t in range(size // 8)])
    for k in range(size):
        home = k // 8
        for rows in tiles:
            held = rows[home]
            row = held[k % 8 : k % 8 + 1, :]
            scaled = row / row[:, k : k + 1]
            for t in range(home, size // 8):
                if t == home and k % 8 == 7:
                    continue
                col = rows[t][:, k : k + 1]
                if t == home:
                    col = jnp.where(sub8 > k % 8, col, 0.0)
                rows[t] = rows[t] - col * scaled
    out = []
    for rows in tiles:
        whole = jnp.concatenate(rows, axis=0)
        diag = jnp.sum(jnp.where(sub == lane, whole[:, :size], 0.0), axis=1, keepdims=True)
        out.append(whole[:, size:] * (1.0 / jnp.sqrt(diag)))
    return out


def mul(a, b, dims):
    return lax.dot_general(a, b, (dims, ((), ())), precision=HIGHEST, preferred_element_type=jnp.float32)


def factor_kernel(inner_ref, out_ref, work):
    modes, rank = inner_ref.shape[0], inner_ref.shape[1]
    sub = lax.broadcasted_iota(jnp.int32, (rank, rank), 0)
    lane = lax.broadcasted_iota(jnp.int32, (rank, rank), 1)
    eye = jnp.where(sub == lane, 1.0, 0.0).astype(jnp.float32)
    for m in range(modes):
        work[m, :, :rank] = inner_ref[m]
        work[m, :, rank:] = eye
    for p in range(rank // BLOCK):
        at = p * BLOCK
        inverses = eliminate([work[m, at : at + BLOCK, at : at + BLOCK] for m in range(modes)])
        for m in range(modes):
            top = mul(inverses[m], work[m, at : at + BLOCK, :], ((1,), (0,)))
            out_ref[m, at : at + BLOCK, :] = top[:, rank:]
            if at + BLOCK < rank:
                left = top[:, at + BLOCK : rank]
                work[m, at + BLOCK :, :] = work[m, at + BLOCK :, :] - mul(left, top, ((0,), (0,)))


def inverse_factors(inner):
    modes, rank = inner.shape[0], inner.shape[1]
    return pl.pallas_call(
        factor_kernel,
        out_shape=jax.ShapeDtypeStruct(inner.shape, jnp.float32),
        in_specs=[pl.BlockSpec(memory_space=pltpu.VMEM)],
        out_specs=pl.BlockSpec(memory_space=pltpu.VMEM),
        scratch_shapes=[pltpu.VMEM((modes, rank, 2 * rank), jnp.float32)],
        name="inverse_factors",
    )(inner)


MESH = pl.DeviceIdType.MESH


def send(src, dst, sems, at, device):
    return pltpu.make_async_remote_copy(
        src_ref=src, dst_ref=dst, send_sem=sems[0].at[at], recv_sem=sems[1].at[at],
        device_id=device, device_id_type=MESH,
    )


def greet(nx, ny, i, j):
    barrier = pltpu.get_barrier_semaphore()
    for d in range(1, ny):
        pl.semaphore_signal(barrier, inc=1, device_id=(i, lax.rem(j + d, ny)), device_id_type=MESH)
    for e in range(1, nx):
        pl.semaphore_signal(barrier, inc=1, device_id=(lax.rem(i + e, nx), j), device_id_type=MESH)
    pl.semaphore_wait(barrier, nx + ny - 2)


def spread(nx, ny, i, j, outs, rows, sems, between=None):
    half = nx // 2
    chip, core = i // 2, lax.rem(i, 2)
    sibling = (i + 1 - 2 * core, j)
    line, plane, pair = sems

    def places(ii, jj):
        spots = (ii * ny + jj, jj * nx + ii)
        return [outs[m].at[pl.ds(pl.multiple_of(spots[m] * rows, rows), rows), :] for m in range(2)]

    sent = []

    def push(block, group, at, device):
        for m in range(2):
            copy = send(block[m], block[m], group, at + (m,), device)
            copy.start()
            sent.append(copy)

    def fan(d):
        jj = lax.rem(j - d + ny, ny)
        block = places(i, jj)
        for e in range(1, half):
            push(block, plane, (e, d), (lax.rem(chip + e, half) * 2 + core, j))
        push(block, pair, (0, d), sibling)

    for d in range(1, ny):
        push(places(i, j), line, (d,), (i, lax.rem(j + d, ny)))
    fan(0)
    if between is not None:
        between()
    for d in range(1, ny):
        for m, block in enumerate(places(i, lax.rem(j - d + ny, ny))):
            send(block, block, line, (d, m), sibling).wait_recv()
        fan(d)
    for d in range(ny):
        for e in range(1, half):
            ii = lax.rem(chip - e + half, half) * 2 + core
            block = places(ii, lax.rem(j - d + ny, ny))
            for m in range(2):
                send(block[m], block[m], plane, (e, d, m), sibling).wait_recv()
            push(block, pair, (e, d), sibling)
    other = i + 1 - 2 * core

    def finish():
        for d in range(ny):
            for e in range(half):
                ii = lax.rem(chip - e + half, half) * 2 + (1 - core)
                block = places(ii, lax.rem(j - d + ny, ny))
                for m in range(2):
                    send(block[m], block[m], pair, (e, d, m), sibling).wait_recv()
        for copy in sent:
            copy.wait_send()

    return finish


def spread_sems(nx, ny):
    half = nx // 2
    shapes = []
    for shape in ((ny, 2), (half, ny, 2), (half, ny, 2)):
        shapes += [pltpu.SemaphoreType.DMA(shape)] * 2
    return shapes


def exchange_kernel(nx, ny, px_ref, py_ref, ox_ref, oy_ref, sx, sy, xs, xr, ys, yr, ls, lr, ps, pr, bs, br):
    i, j = lax.axis_index("gx"), lax.axis_index("gy")
    rows = px_ref.shape[0] // ny
    greet(nx, ny, i, j)

    def part(ref, at):
        return ref.at[pl.ds(pl.multiple_of(at * rows, rows), rows), :]

    copies_x, copies_y = [], []
    for e in range(1, nx):
        to = lax.rem(i + e, nx)
        copies_y.append(send(part(py_ref, to), sy.at[e - 1], (ys, yr), e - 1, (to, j)))
    for d in range(1, ny):
        to = lax.rem(j + d, ny)
        copies_x.append(send(part(px_ref, to), sx.at[d - 1], (xs, xr), d - 1, (i, to)))
    for copy in copies_x + copies_y:
        copy.start()
    for copy in copies_x:
        copy.wait_recv()
    total = part(px_ref, j)[...]
    for d in range(1, ny):
        total = total + sx[d - 1]
    part(ox_ref, i * ny + j)[...] = total
    for copy in copies_y:
        copy.wait_recv()
    total = part(py_ref, i)[...]
    for e in range(1, nx):
        total = total + sy[e - 1]
    part(oy_ref, j * nx + i)[...] = total
    finish = spread(nx, ny, i, j, (ox_ref, oy_ref), rows, ((ls, lr), (ps, pr), (bs, br)))
    finish()
    for copy in copies_x + copies_y:
        copy.wait_send()


def exchange(nx, ny, part_x, part_y):
    rows, rank = part_x.shape[0] // ny, part_x.shape[1]
    whole = jax.ShapeDtypeStruct((rows * nx * ny, rank), jnp.float32)
    dma = pltpu.SemaphoreType.DMA
    return pl.pallas_call(
        functools.partial(exchange_kernel, nx, ny),
        out_shape=(whole, whole),
        in_specs=[pl.BlockSpec(memory_space=pltpu.VMEM)] * 2,
        out_specs=[pl.BlockSpec(memory_space=pltpu.VMEM)] * 2,
        scratch_shapes=[
            pltpu.VMEM((ny - 1, rows, rank), jnp.float32),
            pltpu.VMEM((nx - 1, rows, rank), jnp.float32),
            dma((ny - 1,)), dma((ny - 1,)), dma((nx - 1,)), dma((nx - 1,)),
        ] + spread_sems(nx, ny),
        compiler_params=pltpu.CompilerParams(collective_id=0, has_side_effects=True),
        name="exchange",
    )(part_x, part_y)


def gather_kernel(nx, ny, h_ref, bx_ref, by_ref, hx_ref, hy_ref, ox_ref, oy_ref, own, gs, gr, fs, fr, ks, hs_r, hs_l, hr, ls, lr, ps, pr, bs, br):
    i, j = lax.axis_index("gx"), lax.axis_index("gy")
    half = nx // 2
    chip, core = i // 2, lax.rem(i, 2)
    other = i + 1 - 2 * core
    sibling = (other, j)
    rows = bx_ref.shape[0]
    greet(nx, ny, i, j)
    keep_x = pltpu.make_async_copy(h_ref, hx_ref.at[i], own.at[0])
    keep_y = pltpu.make_async_copy(h_ref, hy_ref.at[j], own.at[1])
    begin_x = pltpu.make_async_copy(bx_ref, ox_ref.at[pl.ds(pl.multiple_of((i * ny + j) * rows, rows), rows), :], own.at[2])
    begin_y = pltpu.make_async_copy(by_ref, oy_ref.at[pl.ds(pl.multiple_of((j * nx + i) * rows, rows), rows), :], own.at[3])
    for copy in (begin_x, begin_y):
        copy.start()
    for copy in (begin_x, begin_y):
        copy.wait()
    waits = []

    def right(src, s):
        return send(src, hy_ref.at[s], (hs_r, hr), s, (i, jnp.minimum(j + 1, ny - 1)))

    def left(src, s):
        return send(src, hy_ref.at[s], (hs_l, hr), s, (i, jnp.maximum(j - 1, 0)))

    def history():
        pl.when(j < ny - 1)(lambda: right(h_ref, j).start())
        pl.when(j > 0)(lambda: left(h_ref, j).start())
        for e in range(1, half):
            copy = send(h_ref, hx_ref.at[i], (gs, gr), e, (lax.rem(chip + e, half) * 2 + core, j))
            copy.start()
            waits.append(copy)
        copy = send(h_ref, hx_ref.at[i], (fs, fr), 0, sibling)
        copy.start()
        waits.append(copy)
        keep_x.start()
        keep_y.start()

    finish = spread(nx, ny, i, j, (ox_ref, oy_ref), rows, ((ls, lr), (ps, pr), (bs, br)), history)
    for d in range(1, ny):
        @pl.when(j - d >= 0)
        def _():
            s = jnp.maximum(j - d, 0)
            right(hy_ref.at[s], s).wait_recv()
            pl.when(j < ny - 1)(lambda: right(hy_ref.at[s], s).start())

        @pl.when(j + d < ny)
        def _():
            s = jnp.minimum(j + d, ny - 1)
            left(hy_ref.at[s], s).wait_recv()
            pl.when(j > 0)(lambda: left(hy_ref.at[s], s).start())
    for e in range(1, half):
        ii = lax.rem(chip - e + half, half) * 2 + core
        send(hx_ref.at[ii], hx_ref.at[ii], (gs, gr), e, sibling).wait_recv()
        copy = send(hx_ref.at[ii], hx_ref.at[ii], (fs, fr), e, sibling)
        copy.start()
        waits.append(copy)
    for e in range(half):
        ii = lax.rem(chip - e + half, half) * 2 + (1 - core)
        send(hx_ref.at[ii], hx_ref.at[ii], (fs, fr), e, sibling).wait_recv()
    finish()
    for copy in waits:
        copy.wait_send()
    for d in range(ny):
        @pl.when(jnp.logical_and(j - d >= 0, j < ny - 1))
        def _():
            s = jnp.maximum(j - d, 0)
            right(hy_ref.at[s], s).wait_send()

        @pl.when(jnp.logical_and(j + d < ny, j > 0))
        def _():
            s = jnp.minimum(j + d, ny - 1)
            left(hy_ref.at[s], s).wait_send()
    keep_x.wait()
    keep_y.wait()


def gather(nx, ny, history, block_x, block_y):
    rows, rank = block_x.shape
    half = nx // 2
    whole = jax.ShapeDtypeStruct((rows * nx * ny, rank), jnp.float32)
    dma = pltpu.SemaphoreType.DMA
    vmem, anywhere = pl.BlockSpec(memory_space=pltpu.VMEM), pl.BlockSpec(memory_space=pl.ANY)
    return pl.pallas_call(
        functools.partial(gather_kernel, nx, ny),
        out_shape=(
            jax.ShapeDtypeStruct((nx,) + history.shape, history.dtype),
            jax.ShapeDtypeStruct((ny,) + history.shape, history.dtype),
            whole, whole,
        ),
        in_specs=[vmem] * 3,
        out_specs=[anywhere, anywhere, vmem, vmem],
        scratch_shapes=[
            dma((4,)), dma((half,)), dma((half,)), dma((half,)), dma((half,)),
            dma((1,)), dma((ny,)), dma((ny,)), dma((ny,)),
        ] + spread_sems(nx, ny),
        compiler_params=pltpu.CompilerParams(collective_id=1, has_side_effects=True),
        name="gather",
    )(history, block_x, block_y)


def dot(a, b, precision):
    return jnp.dot(a, b, precision=precision, preferred_element_type=jnp.float32)


def on_device(history, start_x, start_y):
    nx, ny = lax.axis_size("gx"), lax.axis_size("gy")
    i, j = lax.axis_index("gx"), lax.axis_index("gy")
    rows, cols, rank = history.shape[1], history.shape[2], start_x.shape[1]
    share = rows // ny
    block_x = lax.dynamic_slice_in_dim(start_x, j * share, share, 0)
    block_y = lax.dynamic_slice_in_dim(start_y, i * share, share, 0)
    whole_x, whole_y, basis_x, basis_y = gather(nx, ny, history, block_x, block_y)
    gram_x = lax.dot_general(
        history, whole_x, (((0, 2), (1, 3)), ((), ())), preferred_element_type=jnp.float32
    ).reshape(rows, nx * rows)
    gram_y = lax.dot_general(
        history, whole_y, (((0, 1), (1, 2)), ((), ())), preferred_element_type=jnp.float32
    ).reshape(cols, ny * cols)
    for step in range(ITERS):
        image_x, image_y = exchange(nx, ny, dot(gram_x, basis_x, HIGH), dot(gram_y, basis_y, HIGH))
        inner = jnp.stack([dot(image_x.T, image_x, HIGHEST), dot(image_y.T, image_y, HIGHEST)])
        inverse = inverse_factors(inner)
        if step == ITERS - 1:
            image_x = lax.dynamic_slice_in_dim(image_x, lax.axis_index("gx") * rows, rows, 0)
            image_y = lax.dynamic_slice_in_dim(image_y, lax.axis_index("gy") * cols, cols, 0)
        basis_x = dot(image_x, inverse[0].T, HIGH)
        basis_y = dot(image_y, inverse[1].T, HIGH)
    factor_x = basis_x.astype(jnp.bfloat16)
    factor_y = basis_y.astype(jnp.bfloat16)
    first = jnp.einsum("xa,sxy->say", factor_x, history, preferred_element_type=jnp.float32)
    first = lax.psum_scatter(first, "gx", scatter_dimension=1, tiled=True)
    second = jnp.einsum("say,yb->sab", first, factor_y.astype(jnp.float32), precision=HIGHEST)
    return lax.psum_scatter(second, "gy", scatter_dimension=2, tiled=True)


def solution(mesh):
    return jax.shard_map(
        on_device,
        mesh=mesh,
        in_specs=(P(None, "gx", "gy"), P("gx", None), P("gy", None)),
        out_specs=P(None, "gx", "gy"),
        check_vma=False,
    )
```

```python
import functools

import jax
import jax.numpy as jnp
from jax import lax
from jax.experimental import pallas as pl
from jax.experimental.pallas import tpu as pltpu
from jax.sharding import PartitionSpec as P

ITERS = 3
BLOCK = 64
HIGH = lax.Precision.HIGH
HIGHEST = lax.Precision.HIGHEST


def eliminate(blocks):
    size = blocks[0].shape[0]
    sub = lax.broadcasted_iota(jnp.int32, (size, size), 0)
    lane = lax.broadcasted_iota(jnp.int32, (size, size), 1)
    eye = jnp.where(sub == lane, 1.0, 0.0).astype(jnp.float32)
    sub8 = lax.broadcasted_iota(jnp.int32, (8, 1), 0)
    tiles = []
    for block in blocks:
        whole = jnp.concatenate([block, eye], axis=1)
        tiles.append([whole[t * 8 : t * 8 + 8] for t in range(size // 8)])
    for k in range(size):
        home = k // 8
        for rows in tiles:
            held = rows[home]
            row = held[k % 8 : k % 8 + 1, :]
            scaled = row / row[:, k : k + 1]
            for t in range(home, size // 8):
                if t == home and k % 8 == 7:
                    continue
                col = rows[t][:, k : k + 1]
                if t == home:
                    col = jnp.where(sub8 > k % 8, col, 0.0)
                rows[t] = rows[t] - col * scaled
    out = []
    for rows in tiles:
        whole = jnp.concatenate(rows, axis=0)
        diag = jnp.sum(jnp.where(sub == lane, whole[:, :size], 0.0), axis=1, keepdims=True)
        out.append(whole[:, size:] * (1.0 / jnp.sqrt(diag)))
    return out


def mul(a, b, dims):
    return lax.dot_general(a, b, (dims, ((), ())), precision=HIGHEST, preferred_element_type=jnp.float32)


def factor_kernel(inner_ref, out_ref, work):
    modes, rank = inner_ref.shape[0], inner_ref.shape[1]
    sub = lax.broadcasted_iota(jnp.int32, (rank, rank), 0)
    lane = lax.broadcasted_iota(jnp.int32, (rank, rank), 1)
    eye = jnp.where(sub == lane, 1.0, 0.0).astype(jnp.float32)
    for m in range(modes):
        work[m, :, :rank] = inner_ref[m]
        work[m, :, rank:] = eye
    for p in range(rank // BLOCK):
        at = p * BLOCK
        inverses = eliminate([work[m, at : at + BLOCK, at : at + BLOCK] for m in range(modes)])
        for m in range(modes):
            top = mul(inverses[m], work[m, at : at + BLOCK, :], ((1,), (0,)))
            out_ref[m, at : at + BLOCK, :] = top[:, rank:]
            if at + BLOCK < rank:
                left = top[:, at + BLOCK : rank]
                work[m, at + BLOCK :, :] = work[m, at + BLOCK :, :] - mul(left, top, ((0,), (0,)))


def inverse_factors(inner):
    modes, rank = inner.shape[0], inner.shape[1]
    return pl.pallas_call(
        factor_kernel,
        out_shape=jax.ShapeDtypeStruct(inner.shape, jnp.float32),
        in_specs=[pl.BlockSpec(memory_space=pltpu.VMEM)],
        out_specs=pl.BlockSpec(memory_space=pltpu.VMEM),
        scratch_shapes=[pltpu.VMEM((modes, rank, 2 * rank), jnp.float32)],
        name="inverse_factors",
    )(inner)


MESH = pl.DeviceIdType.MESH


def send(src, dst, sems, at, device):
    return pltpu.make_async_remote_copy(
        src_ref=src, dst_ref=dst, send_sem=sems[0].at[at], recv_sem=sems[1].at[at],
        device_id=device, device_id_type=MESH,
    )


def greet(nx, ny, i, j):
    barrier = pltpu.get_barrier_semaphore()
    for d in range(1, ny):
        pl.semaphore_signal(barrier, inc=1, device_id=(i, lax.rem(j + d, ny)), device_id_type=MESH)
    for e in range(1, nx):
        pl.semaphore_signal(barrier, inc=1, device_id=(lax.rem(i + e, nx), j), device_id_type=MESH)
    pl.semaphore_wait(barrier, nx + ny - 2)


def spread(nx, ny, i, j, outs, rows, sems, between=None, middle=None):
    half = nx // 2
    chip, core = i // 2, lax.rem(i, 2)
    sibling = (i + 1 - 2 * core, j)
    line, plane, pair = sems

    def places(ii, jj):
        spots = (ii * ny + jj, jj * nx + ii)
        return [outs[m].at[pl.ds(pl.multiple_of(spots[m] * rows, rows), rows), :] for m in range(2)]

    sent = []

    def push(block, group, at, device):
        for m in range(2):
            copy = send(block[m], block[m], group, at + (m,), device)
            copy.start()
            sent.append(copy)

    def fan(d):
        jj = lax.rem(j - d + ny, ny)
        block = places(i, jj)
        for e in range(1, half):
            push(block, plane, (e, d), (lax.rem(chip + e, half) * 2 + core, j))
        push(block, pair, (0, d), sibling)

    for d in range(1, ny):
        push(places(i, j), line, (d,), (i, lax.rem(j + d, ny)))
    fan(0)
    if between is not None:
        between()
    for d in range(1, ny):
        for m, block in enumerate(places(i, lax.rem(j - d + ny, ny))):
            send(block, block, line, (d, m), sibling).wait_recv()
        fan(d)
    if middle is not None:
        middle()
    for d in range(ny):
        for e in range(1, half):
            ii = lax.rem(chip - e + half, half) * 2 + core
            block = places(ii, lax.rem(j - d + ny, ny))
            for m in range(2):
                send(block[m], block[m], plane, (e, d, m), sibling).wait_recv()
            push(block, pair, (e, d), sibling)

    def finish():
        for d in range(ny):
            for e in range(half):
                ii = lax.rem(chip - e + half, half) * 2 + (1 - core)
                block = places(ii, lax.rem(j - d + ny, ny))
                for m in range(2):
                    send(block[m], block[m], pair, (e, d, m), sibling).wait_recv()
        for copy in sent:
            copy.wait_send()

    return finish


def spread_sems(nx, ny):
    half = nx // 2
    shapes = []
    for shape in ((ny, 2), (half, ny, 2), (half, ny, 2)):
        shapes += [pltpu.SemaphoreType.DMA(shape)] * 2
    return shapes


def exchange_kernel(nx, ny, px_ref, py_ref, ox_ref, oy_ref, sx, sy, xs, xr, ys, yr, ls, lr, ps, pr, bs, br):
    i, j = lax.axis_index("gx"), lax.axis_index("gy")
    rows = px_ref.shape[0] // ny
    greet(nx, ny, i, j)

    def part(ref, at):
        return ref.at[pl.ds(pl.multiple_of(at * rows, rows), rows), :]

    copies_x, copies_y = [], []
    for e in range(1, nx):
        to = lax.rem(i + e, nx)
        copies_y.append(send(part(py_ref, to), sy.at[e - 1], (ys, yr), e - 1, (to, j)))
    for d in range(1, ny):
        to = lax.rem(j + d, ny)
        copies_x.append(send(part(px_ref, to), sx.at[d - 1], (xs, xr), d - 1, (i, to)))
    for copy in copies_x + copies_y:
        copy.start()
    for copy in copies_x:
        copy.wait_recv()
    total = part(px_ref, j)[...]
    for d in range(1, ny):
        total = total + sx[d - 1]
    part(ox_ref, i * ny + j)[...] = total
    for copy in copies_y:
        copy.wait_recv()
    total = part(py_ref, i)[...]
    for e in range(1, nx):
        total = total + sy[e - 1]
    part(oy_ref, j * nx + i)[...] = total
    finish = spread(nx, ny, i, j, (ox_ref, oy_ref), rows, ((ls, lr), (ps, pr), (bs, br)))
    finish()
    for copy in copies_x + copies_y:
        copy.wait_send()


def exchange(nx, ny, part_x, part_y):
    rows, rank = part_x.shape[0] // ny, part_x.shape[1]
    whole = jax.ShapeDtypeStruct((rows * nx * ny, rank), jnp.float32)
    dma = pltpu.SemaphoreType.DMA
    return pl.pallas_call(
        functools.partial(exchange_kernel, nx, ny),
        out_shape=(whole, whole),
        in_specs=[pl.BlockSpec(memory_space=pltpu.VMEM)] * 2,
        out_specs=[pl.BlockSpec(memory_space=pltpu.VMEM)] * 2,
        scratch_shapes=[
            pltpu.VMEM((ny - 1, rows, rank), jnp.float32),
            pltpu.VMEM((nx - 1, rows, rank), jnp.float32),
            dma((ny - 1,)), dma((ny - 1,)), dma((nx - 1,)), dma((nx - 1,)),
        ] + spread_sems(nx, ny),
        compiler_params=pltpu.CompilerParams(collective_id=0, has_side_effects=True),
        name="exchange",
    )(part_x, part_y)


def gather_kernel(nx, ny, h_ref, bx_ref, by_ref, hx_ref, hy_ref, ox_ref, oy_ref, own, gs, gr, fs, fr, ks, hs_r, hs_l, hr, ls, lr, ps, pr, bs, br):
    i, j = lax.axis_index("gx"), lax.axis_index("gy")
    half = nx // 2
    chip, core = i // 2, lax.rem(i, 2)
    other = i + 1 - 2 * core
    sibling = (other, j)
    rows = bx_ref.shape[0]
    greet(nx, ny, i, j)
    keep_x = pltpu.make_async_copy(h_ref, hx_ref.at[i], own.at[0])
    keep_y = pltpu.make_async_copy(h_ref, hy_ref.at[j], own.at[1])
    begin_x = pltpu.make_async_copy(bx_ref, ox_ref.at[pl.ds(pl.multiple_of((i * ny + j) * rows, rows), rows), :], own.at[2])
    begin_y = pltpu.make_async_copy(by_ref, oy_ref.at[pl.ds(pl.multiple_of((j * nx + i) * rows, rows), rows), :], own.at[3])
    for copy in (begin_x, begin_y):
        copy.start()
    for copy in (begin_x, begin_y):
        copy.wait()
    waits = []

    def right(src, s):
        return send(src, hy_ref.at[s], (hs_r, hr), s, (i, jnp.minimum(j + 1, ny - 1)))

    def left(src, s):
        return send(src, hy_ref.at[s], (hs_l, hr), s, (i, jnp.maximum(j - 1, 0)))

    def history():
        pl.when(j < ny - 1)(lambda: right(h_ref, j).start())
        pl.when(j > 0)(lambda: left(h_ref, j).start())
        for e in range(1, half):
            copy = send(h_ref, hx_ref.at[i], (gs, gr), e, (lax.rem(chip + e, half) * 2 + core, j))
            copy.start()
            waits.append(copy)
        copy = send(h_ref, hx_ref.at[i], (fs, fr), 0, sibling)
        copy.start()
        waits.append(copy)
        keep_x.start()
        keep_y.start()

    def relay(d):
        @pl.when(j - d >= 0)
        def _():
            s = jnp.maximum(j - d, 0)
            right(hy_ref.at[s], s).wait_recv()
            pl.when(j < ny - 1)(lambda: right(hy_ref.at[s], s).start())

        @pl.when(j + d < ny)
        def _():
            s = jnp.minimum(j + d, ny - 1)
            left(hy_ref.at[s], s).wait_recv()
            pl.when(j > 0)(lambda: left(hy_ref.at[s], s).start())

    def relays():
        for d in range(1, ny - 1):
            relay(d)

    sems = ((ls, lr), (ps, pr), (bs, br))
    finish = spread(nx, ny, i, j, (ox_ref, oy_ref), rows, sems, history, relays)
    for e in range(1, half):
        ii = lax.rem(chip - e + half, half) * 2 + core
        send(hx_ref.at[ii], hx_ref.at[ii], (gs, gr), e, sibling).wait_recv()
        copy = send(hx_ref.at[ii], hx_ref.at[ii], (fs, fr), e, sibling)
        copy.start()
        waits.append(copy)
    for e in range(half):
        ii = lax.rem(chip - e + half, half) * 2 + (1 - core)
        send(hx_ref.at[ii], hx_ref.at[ii], (fs, fr), e, sibling).wait_recv()
    if ny > 1:
        relay(ny - 1)
    finish()
    for copy in waits:
        copy.wait_send()
    for d in range(ny):
        @pl.when(jnp.logical_and(j - d >= 0, j < ny - 1))
        def _():
            s = jnp.maximum(j - d, 0)
            right(hy_ref.at[s], s).wait_send()

        @pl.when(jnp.logical_and(j + d < ny, j > 0))
        def _():
            s = jnp.minimum(j + d, ny - 1)
            left(hy_ref.at[s], s).wait_send()
    keep_x.wait()
    keep_y.wait()


def gather(nx, ny, history, block_x, block_y):
    rows, rank = block_x.shape
    half = nx // 2
    whole = jax.ShapeDtypeStruct((rows * nx * ny, rank), jnp.float32)
    dma = pltpu.SemaphoreType.DMA
    vmem, anywhere = pl.BlockSpec(memory_space=pltpu.VMEM), pl.BlockSpec(memory_space=pl.ANY)
    return pl.pallas_call(
        functools.partial(gather_kernel, nx, ny),
        out_shape=(
            jax.ShapeDtypeStruct((nx,) + history.shape, history.dtype),
            jax.ShapeDtypeStruct((ny,) + history.shape, history.dtype),
            whole, whole,
        ),
        in_specs=[vmem] * 3,
        out_specs=[anywhere, anywhere, vmem, vmem],
        scratch_shapes=[
            dma((4,)), dma((half,)), dma((half,)), dma((half,)), dma((half,)),
            dma((1,)), dma((ny,)), dma((ny,)), dma((ny,)),
        ] + spread_sems(nx, ny),
        compiler_params=pltpu.CompilerParams(collective_id=1, has_side_effects=True),
        name="gather",
    )(history, block_x, block_y)


def settle_kernel(ny, part_ref, out_ref, slots, ss, sr):
    i, j = lax.axis_index("gx"), lax.axis_index("gy")
    barrier = pltpu.get_barrier_semaphore()
    for d in range(1, ny):
        pl.semaphore_signal(barrier, inc=1, device_id=(i, lax.rem(j + d, ny)), device_id_type=MESH)
    pl.semaphore_wait(barrier, ny - 1)
    copies = []
    for d in range(1, ny):
        to = lax.rem(j + d, ny)
        copies.append(send(part_ref.at[to], slots.at[d - 1], (ss, sr), d - 1, (i, to)))
    for copy in copies:
        copy.start()
    for copy in copies:
        copy.wait_recv()
    total = part_ref[j]
    for d in range(1, ny):
        total = total + slots[d - 1]
    out_ref[...] = total
    for copy in copies:
        copy.wait_send()


def settle(ny, part):
    block = part.shape[1:]
    dma = pltpu.SemaphoreType.DMA
    return pl.pallas_call(
        functools.partial(settle_kernel, ny),
        out_shape=jax.ShapeDtypeStruct(block, jnp.float32),
        in_specs=[pl.BlockSpec(memory_space=pltpu.VMEM)],
        out_specs=pl.BlockSpec(memory_space=pltpu.VMEM),
        scratch_shapes=[pltpu.VMEM((ny - 1,) + block, jnp.float32), dma((ny - 1,)), dma((ny - 1,))],
        compiler_params=pltpu.CompilerParams(collective_id=2, has_side_effects=True),
        name="settle",
    )(part)


def dot(a, b, precision):
    return jnp.dot(a, b, precision=precision, preferred_element_type=jnp.float32)


def on_device(history, start_x, start_y):
    nx, ny = lax.axis_size("gx"), lax.axis_size("gy")
    i, j = lax.axis_index("gx"), lax.axis_index("gy")
    rows, cols, rank = history.shape[1], history.shape[2], start_x.shape[1]
    share = rows // ny
    block_x = lax.dynamic_slice_in_dim(start_x, j * share, share, 0)
    block_y = lax.dynamic_slice_in_dim(start_y, i * share, share, 0)
    whole_x, whole_y, basis_x, basis_y = gather(nx, ny, history, block_x, block_y)
    gram_x = lax.dot_general(
        history, whole_x, (((0, 2), (1, 3)), ((), ())), preferred_element_type=jnp.float32
    ).reshape(rows, nx * rows)
    gram_y = lax.dot_general(
        history, whole_y, (((0, 1), (1, 2)), ((), ())), preferred_element_type=jnp.float32
    ).reshape(cols, ny * cols)
    for step in range(ITERS):
        image_x, image_y = exchange(nx, ny, dot(gram_x, basis_x, HIGH), dot(gram_y, basis_y, HIGH))
        inner = jnp.stack([dot(image_x.T, image_x, HIGHEST), dot(image_y.T, image_y, HIGHEST)])
        inverse = inverse_factors(inner)
        turn_x = inverse[0].T
        if step == ITERS - 1:
            turn_x = lax.dynamic_slice_in_dim(turn_x, i * (rank // nx), rank // nx, 1)
            image_y = lax.dynamic_slice_in_dim(image_y, j * cols, cols, 0)
        basis_x = dot(image_x, turn_x, HIGH)
        basis_y = dot(image_y, inverse[1].T, HIGH)
    factor_x = basis_x.astype(jnp.bfloat16).reshape(nx, rows, rank // nx)
    factor_y = basis_y.astype(jnp.bfloat16)
    first = jnp.einsum("ixa,isxy->say", factor_x, whole_x, preferred_element_type=jnp.float32)
    wide = factor_y.astype(jnp.float32).reshape(cols, ny, rank // ny)
    second = jnp.einsum("say,ynb->nsab", first, wide, precision=HIGHEST)
    slabs = second.shape[1]
    core = settle(ny, second.reshape(ny, -1, rank // ny))
    return core.reshape(slabs, rank // nx, rank // ny)


def solution(mesh):
    return jax.shard_map(
        on_device,
        mesh=mesh,
        in_specs=(P(None, "gx", "gy"), P("gx", None), P("gy", None)),
        out_specs=P(None, "gx", "gy"),
        check_vma=False,
    )
```
